128 devices in a mesh: expert: 32 (over y, x, core), dp: 4 (over z).
Axes of the slice: x: 4, y: 4, z: 4, core: 2. Of those that a mesh axis runs over, the one named last changes fastest.
Arguments:
- tokens: bfloat16 [4096, 4096], P('expert', 'dp'), may hold values from -6 to 6
- cotangent: bfloat16 [4096, 4096], P('expert', 'dp'), may hold values from -6 to 6
- gate_probs: bfloat16 [4096, 8], P('expert'), may hold values from 0.019897461 to 0.3984375
- expert_ids: int32 [4096, 8], P('expert'), may hold values from 0 to 31, all different within a row; in each aligned block of 128 rows (0 to 127, 128 to 255, ...) at most 36 rows name the same one
- gate_weight: bfloat16 [32, 4096, 1024], P('expert', 'dp'), may hold values from -0.09375 to 0.09375
- up_weight: bfloat16 [32, 4096, 1024], P('expert', 'dp'), may hold values from -0.09375 to 0.09375
- down_weight: bfloat16 [32, 1024, 4096], P('expert', None, 'dp'), may hold values from -0.1875 to 0.1875
Outputs:
- grad_tokens: bfloat16 [4096, 4096], P('expert', 'dp')
- grad_gates: float32 [4096, 8], P('expert')
- grad_gate_weight: float32 [32, 4096, 1024], P('expert', 'dp')
- grad_up_weight: float32 [32, 4096, 1024], P('expert', 'dp')
- grad_down_weight: float32 [32, 1024, 4096], P('expert', None, 'dp')
The draws below stay inside these ranges and needn't reach their ends.
Inputs may be any that keep to these rules, and one draw needn't show every extreme that they name: `expert_ids`: each row names 8 different experts. Among the 128 rows of one group no expert is named more than 36 times, and in every draw some expert is named exactly 36 times by the rows of some group.
All inputs are finite; a program needn't handle non-finite values.
Results may differ from the reference program's by a relative error of at most 0.012.
Values may be sent and summed in bfloat16 or wider, within the bound.
A program may use at most 128 MiB of HBM per device.

```python
import math
import jax
import jax.numpy as jnp
import numpy as np
from jax import lax

D = 4096
FF = 1024
TOP = 8
EXPERTS = 32
TOK_GRP = 128
CAP = 36
TOKENS = 4096
N_EXPERT = 32
N_DP = 4


def steps_of(rng, dims, shards, least, high):
    def one(axis_at, parts):
        draws = jax.random.uniform(jax.random.fold_in(jax.random.fold_in(rng, 6), axis_at), (parts,), jnp.float32, least / len(shards), high / len(shards))
        return jnp.repeat(jnp.exp(draws), dims[axis_at] // parts).reshape((-1,) + (1,) * (len(dims) - axis_at - 1))

    level = one(*shards[0])
    for cut in shards[1:]:
        level = level * one(*cut)
    return level


def assign_block(own_key, own, number, rows, amount, top, bound, slope):
    sequence = jax.random.permutation(own_key, amount)
    crowded, common = portions_of(amount, rows * top, bound, slope, True), portions_of(amount, rows * top, bound, slope, False)
    places = jnp.arange(amount)

    def named(lengths, offset_by):
        used = int((lengths > 0).sum())
        fixed = max(1, used // 4)
        shifted = fixed + (places - fixed + offset_by * (used - fixed)) % max(1, amount - fixed)
        return jnp.zeros((amount,), jnp.int32).at[sequence[jnp.where(places < fixed, places, shifted)]].set(jnp.asarray(lengths, jnp.int32))

    lengths = jnp.where(number % 4 == 0, named(crowded, number // 4), named(common, number - number // 4 - 1))
    mixed = jax.random.permutation(jax.random.fold_in(own, 3), amount)
    giver, receiver = mixed[0:amount // 2 * 2:2], mixed[1:amount // 2 * 2:2]
    margin = jnp.minimum(lengths[giver] - 1, bound - lengths[receiver]) // 2
    margin = jnp.where((giver == sequence[0]) | (receiver == sequence[0]) | (lengths[receiver] == 0), 0, jnp.maximum(margin, 0))
    shifted = jax.random.randint(jax.random.fold_in(own, 4), (amount // 2,), 0, 1 << 20) % (margin + 1)
    lengths = lengths.at[giver].add(-shifted).at[receiver].add(shifted)
    members = jnp.searchsorted(jnp.cumsum(lengths), jnp.arange(rows * top), side="right").astype(jnp.int32)
    listing = members.reshape(top, rows).T
    listing = listing[jax.random.permutation(jax.random.fold_in(own, 1), rows)]
    offset_by = jax.random.randint(jax.random.fold_in(own, 2), (rows, 1), 0, top)
    return jnp.take_along_axis(listing, (jnp.arange(top)[None, :] + offset_by) % top, axis=1)


def portions_of(amount, total, reach, slope, full):
    loads = [(1 << 20) // math.isqrt(standing ** slope) + 1 for standing in range(1, amount + 1)]
    largest = reach if full else min(reach, max(-(-total // amount), total * loads[0] // sum(loads)))
    least = 1 if total - largest >= amount - 1 else 0
    holding, surplus = [largest] + [least] * (amount - 1), total - largest - least * (amount - 1)
    while surplus > 0:
        movable = [i for i in range(1, amount) if holding[i] < largest] or [i for i in range(1, amount) if holding[i] < reach]
        pool, left = sum([loads[i] for i in movable]), surplus
        for i in movable:
            addition = min(reach - holding[i], max(1, left * loads[i] // pool), surplus)
            holding[i] = holding[i] + addition
            surplus = surplus - addition
    return np.array(holding)


def scatter_about(key, extent, width, bound, split=(), kind=jnp.bfloat16):
    drawn = jax.random.normal(key, extent, jnp.float32) * width
    if len(split) > 0:
        drawn = steps_of(key, extent, split, -0.22, 0.18) * drawn
    return jnp.clip(drawn, min=-bound, max=bound).astype(kind)


def setup_inputs(seed: int = 0) -> dict:
    key_of = jax.random.split(jax.random.key(seed), 8)
    tokens = scatter_about(key_of[0], (TOKENS, D), 1.0, 6.0, ((0, 32), (1, 4)))
    cotangent = scatter_about(key_of[1], (TOKENS, D), 1.0, 6.0, ((0, 32), (1, 4)))
    gate_probs = jnp.clip(jnp.exp(math.log(0.3984375) - 2.9969585 * jax.random.uniform(key_of[2], (TOKENS, TOP), jnp.float32) ** steps_of(key_of[2], (TOKENS, TOP), ((0, 32),), -0.2, 0.2)), 0.019897461, 0.3984375).astype(jnp.bfloat16)
    expert_ids_keys = jax.random.split(jax.random.fold_in(key_of[3], 1), TOKENS // TOK_GRP)
    expert_ids_turns = jax.random.permutation(jax.random.fold_in(key_of[3], 3), TOKENS // TOK_GRP)
    expert_ids = jax.vmap(lambda own, number: assign_block(jax.random.fold_in(key_of[3], 2), own, number, TOK_GRP, EXPERTS, TOP, CAP, 2))(expert_ids_keys, expert_ids_turns).reshape((TOKENS, TOP))
    gate_weight = scatter_about(key_of[4], (EXPERTS, D, FF), D ** -0.5, 0.09375, ((0, 32), (1, 4)))
    up_weight = scatter_about(key_of[5], (EXPERTS, D, FF), D ** -0.5, 0.09375, ((0, 32), (1, 4)))
    down_weight = scatter_about(key_of[6], (EXPERTS, FF, D), FF ** -0.5, 0.1875, ((0, 32), (2, 4)))
    return dict(tokens=tokens, cotangent=cotangent, gate_probs=gate_probs, expert_ids=expert_ids, gate_weight=gate_weight, up_weight=up_weight, down_weight=down_weight)


def expert_reference(operands):
    x_rows, dy_rows, g_rows, gate_w, up_w, down_w = operands
    row_count = x_rows.shape[0]
    gate_pre = jnp.dot(x_rows, gate_w, preferred_element_type=jnp.float32)
    up_pre = jnp.dot(x_rows, up_w, preferred_element_type=jnp.float32)
    back_hidden = jnp.dot(dy_rows, down_w.T, preferred_element_type=jnp.float32)
    sigmoid_gate = jax.nn.sigmoid(gate_pre)
    swish_gate = gate_pre * sigmoid_gate
    hidden = (swish_gate * up_pre).astype(jnp.bfloat16)
    gate_blocks = (back_hidden * hidden.astype(jnp.float32)).reshape(row_count, N_DP, FF // N_DP).sum(-1)
    gate_terms = lax.optimization_barrier(gate_blocks.astype(jnp.bfloat16)).astype(jnp.float32).sum(-1)
    scaled = g_rows.astype(jnp.float32)[:, None]
    grad_hidden = scaled * back_hidden
    derivative = sigmoid_gate * (1.0 + gate_pre * (1.0 - sigmoid_gate))
    grad_gate_pre = (grad_hidden * up_pre * derivative).astype(jnp.bfloat16)
    grad_up_pre = (grad_hidden * swish_gate).astype(jnp.bfloat16)
    input_terms = jnp.dot(grad_gate_pre, gate_w.T, preferred_element_type=jnp.float32)
    input_terms = input_terms + jnp.dot(grad_up_pre, up_w.T, preferred_element_type=jnp.float32)
    input_part = input_terms.astype(jnp.bfloat16)
    scaled_dy = (scaled * dy_rows.astype(jnp.float32)).astype(jnp.bfloat16)
    grad_down = jnp.dot(hidden.T, scaled_dy, preferred_element_type=jnp.float32)
    grad_gate = jnp.dot(x_rows.T, grad_gate_pre, preferred_element_type=jnp.float32)
    grad_up = jnp.dot(x_rows.T, grad_up_pre, preferred_element_type=jnp.float32)
    return input_part, gate_terms, grad_gate, grad_up, grad_down


def reference(tokens, cotangent, gate_probs, expert_ids, gate_weight, up_weight, down_weight):
    group_total = N_EXPERT
    per_group = expert_ids.reshape(group_total, TOK_GRP * TOP)
    columns = jnp.arange(EXPERTS, dtype=jnp.int32)
    member = (per_group[:, :, None] == columns[None, None, :]).astype(jnp.int32)
    ranked = jnp.cumsum(member, axis=1) - 1
    within = jnp.sum(member * ranked, axis=2).astype(jnp.int32)
    group_index = jnp.arange(group_total, dtype=jnp.int32)[:, None]
    position = (group_index * CAP + within).reshape(-1).astype(jnp.int32)
    flat_ids = expert_ids.reshape(-1).astype(jnp.int32)
    row_total = group_total * CAP
    x_repeat = jnp.repeat(tokens, TOP, axis=0)
    dy_repeat = jnp.repeat(cotangent, TOP, axis=0)
    x_buffer = jnp.zeros((EXPERTS, row_total, D), jnp.bfloat16).at[flat_ids, position].set(x_repeat)
    dy_buffer = jnp.zeros((EXPERTS, row_total, D), jnp.bfloat16).at[flat_ids, position].set(dy_repeat)
    g_buffer = jnp.zeros((EXPERTS, row_total), jnp.bfloat16).at[flat_ids, position].set(gate_probs.reshape(-1))
    input_parts, gate_terms, grad_gate, grad_up, grad_down = lax.map(
        expert_reference, (x_buffer, dy_buffer, g_buffer, gate_weight, up_weight, down_weight))
    picked = lax.optimization_barrier(input_parts[flat_ids, position]).astype(jnp.float32)
    grad_tokens = picked.reshape(TOKENS, TOP, D).sum(1).astype(jnp.bfloat16)
    grad_gates = gate_terms[flat_ids, position].reshape(TOKENS, TOP)
    return grad_tokens, grad_gates, grad_gate, grad_up, grad_down
```

```python
import jax
import jax.numpy as jnp
from jax import lax
from jax.sharding import PartitionSpec as P

TOP = 8
EXPERTS = 32
CAP = 36


def dot32(spec, a, b):
    return jnp.einsum(spec, a, b, preferred_element_type=jnp.float32)


def hidden_units(gate_pre, up_pre, back_hidden, g_rows):
    sigmoid_gate = jax.nn.sigmoid(gate_pre)
    swish_gate = gate_pre * sigmoid_gate
    hidden = (swish_gate * up_pre).astype(jnp.bfloat16)
    product = back_hidden * hidden.astype(jnp.float32)
    grad_hidden = g_rows * back_hidden
    derivative = sigmoid_gate * (1.0 + gate_pre * (1.0 - sigmoid_gate))
    grad_gate_pre = (grad_hidden * up_pre * derivative).astype(jnp.bfloat16)
    grad_up_pre = (grad_hidden * swish_gate).astype(jnp.bfloat16)
    return (hidden, grad_gate_pre, grad_up_pre, product)


def shards(tokens, cotangent, gate_probs, expert_ids, gate_weight, up_weight, down_weight):
    me = lax.axis_index("expert")
    groups = lax.axis_size("expert")
    count, width = tokens.shape
    wg, wu, wd = gate_weight[0], up_weight[0], down_weight[0]
    columns = jnp.arange(128, dtype=jnp.int32)
    chosen = expert_ids[:, :, None] == columns[None, None, :]
    routed = jnp.sum(jnp.where(chosen, gate_probs[:, :, None].astype(jnp.float32), 0.0), axis=1)
    routed = routed.astype(jnp.bfloat16)
    everything = lax.all_gather(
        jnp.concatenate([tokens, cotangent, routed], axis=1), "expert", axis=0, tiled=False
    )
    x_all, dy_all = everything[:, :, :width], everything[:, :, width : 2 * width]
    mine = jnp.sum(
        jnp.where(columns[None, None, :] == me, everything[:, :, 2 * width :], 0), axis=2
    )
    before = (jnp.arange(count)[:, None] < jnp.arange(count)[None, :]).astype(jnp.bfloat16)
    member = (mine > 0).astype(jnp.bfloat16)
    rank = dot32("gt,tu->gu", member, before)
    slots = jnp.arange(CAP, dtype=jnp.float32)
    pick = (rank[:, None, :] == slots[None, :, None]) & (mine[:, None, :] > 0)
    g_rows = jnp.sum(jnp.where(pick, mine[:, None, :].astype(jnp.float32), 0.0), axis=2)
    pick = pick.astype(jnp.bfloat16)
    rows = groups * CAP
    x_rows = dot32("gst,gtd->gsd", pick, x_all).astype(jnp.bfloat16).reshape(rows, width)
    dy_rows = dot32("gst,gtd->gsd", pick, dy_all).astype(jnp.bfloat16).reshape(rows, width)
    g_rows = g_rows.reshape(rows, 1)
    parts = (
        dot32("rd,df->rf", x_rows, wg).astype(jnp.bfloat16),
        dot32("rd,df->rf", x_rows, wu).astype(jnp.bfloat16),
        dot32("rd,fd->rf", dy_rows, wd).astype(jnp.bfloat16),
    )
    gate_pre, up_pre, back_hidden = (
        lax.psum_scatter(part, "dp", scatter_dimension=1, tiled=True).astype(jnp.float32)
        for part in parts
    )
    hidden, grad_gate_pre, grad_up_pre, product = hidden_units(
        gate_pre, up_pre, back_hidden, g_rows
    )
    block_sum = jnp.sum(product, axis=1, keepdims=True).astype(jnp.bfloat16)
    hidden, grad_gate_pre, grad_up_pre, gate_blocks = (
        lax.all_gather(part, "dp", axis=1, tiled=True)
        for part in (hidden, grad_gate_pre, grad_up_pre, block_sum)
    )
    input_part = dot32("rf,df->rd", grad_gate_pre, wg) + dot32("rf,df->rd", grad_up_pre, wu)
    input_part = input_part.astype(jnp.bfloat16)
    scaled_dy = (dy_rows.astype(jnp.float32) * g_rows).astype(jnp.bfloat16)
    grad_down = dot32("rf,rd->fd", hidden, scaled_dy)
    grad_gate = dot32("rd,rf->df", x_rows, grad_gate_pre)
    grad_up = dot32("rd,rf->df", x_rows, grad_up_pre)
    input_table = lax.all_to_all(
        input_part.reshape(groups, CAP, width), "expert", split_axis=0, concat_axis=0
    )
    gate_table = lax.all_to_all(
        gate_blocks.reshape(groups, CAP, -1), "expert", split_axis=0, concat_axis=0
    )
    gate_table = jnp.sum(gate_table.astype(jnp.float32), axis=2)
    local = routed[:, :EXPERTS]
    local_rank = dot32("tu,te->ue", before, (local > 0).astype(jnp.bfloat16))
    place = (local_rank[:, :, None] == slots[None, None, :]) & (local[:, :, None] > 0)
    by_expert = jnp.sum(jnp.where(place, gate_table[None], 0.0), axis=2)
    grad_gates = jnp.sum(jnp.where(chosen[:, :, :EXPERTS], by_expert[:, None, :], 0.0), axis=2)
    place = place.astype(jnp.bfloat16).reshape(count, rows)
    grad_tokens = dot32("tr,rd->td", place, input_table.reshape(rows, width)).astype(jnp.bfloat16)
    return (grad_tokens, grad_gates, grad_gate[None], grad_up[None], grad_down[None])


def solution(mesh):
    placed = (
        P("expert", "dp"),
        P("expert", "dp"),
        P("expert", None),
        P("expert", None),
        P("expert", "dp", None),
        P("expert", "dp", None),
        P("expert", None, "dp"),
    )
    return jax.shard_map(
        shards,
        mesh=mesh,
        in_specs=placed,
        out_specs=(
            P("expert", "dp"),
            P("expert", None),
            P("expert", "dp", None),
            P("expert", "dp", None),
            P("expert", None, "dp"),
        ),
        check_vma=False,
    )
```

```python
import functools

import jax
import jax.numpy as jnp
from jax import lax
from jax.experimental import pallas as pl
from jax.experimental.pallas import tpu as pltpu
from jax.sharding import PartitionSpec as P

EXPERTS = 32
CAP = 36
PAD = 40
HALF = 4 * CAP
ORDER = (0, 1, 3, 2)
BF = jnp.bfloat16
F32 = jnp.float32
MESH = pl.DeviceIdType.MESH
NT = (((1,), (1,)), ((), ()))
TN = (((0,), (0,)), ((), ()))


def dot32(spec, a, b):
    return jnp.einsum(spec, a, b, preferred_element_type=F32)


def mm(a, b):
    return jnp.dot(a, b, preferred_element_type=F32)


def mm_nt(a, b):
    return lax.dot_general(a, b, NT, preferred_element_type=F32)


def mm_tn(a, b):
    return lax.dot_general(a, b, TN, preferred_element_type=F32)


def landed(ref, sem):
    pltpu.make_async_copy(ref, ref, sem).wait()


def layer_kernel(
    tok_in, cot_in, routed_in, wg_in, wu_in, wd_in,
    xr_out, sdy_out, act_out, ret_out,
    tok, wg, wu, wd, routed, pick, g_rows, xr, sdy, dyr, part, r1, r2, act, prod, gates, inp, ret,
    own_sem, tok_s, tok_r, routed_s, routed_r, r1_s, r1_r, r2_s, r2_r, ag_s, ag_r,
    gates_s, gates_r, ret_s, ret_r, out_s,
):
    me = lax.axis_index("expert")
    z = lax.axis_index("dp")
    core = lax.rem(me, 2)
    chip_x = lax.rem(me // 2, 4)
    chip_y = me // 8
    a = chip_x * (1 - core) + chip_y * core
    b = chip_y * (1 - core) + chip_x * core

    def holder(side, da, db):
        kind = core if side == 0 else 1 - core
        first, second = (a, b) if side == 0 else (b, a)
        first, second = lax.rem(first + da, 4), lax.rem(second + db, 4)
        return ((1 - kind) * (second * 4 + first) + kind * (first * 4 + second)) * 2 + kind

    def plane(index):
        return {"expert": index}

    def column(step):
        return {"dp": lax.rem(z + step, 4)}

    partner = plane(me + 1 - 2 * core)
    sent = []

    def send(src, dst, ssem, rsem, device):
        copy = pltpu.make_async_remote_copy(
            src_ref=src, dst_ref=dst, send_sem=ssem, recv_sem=rsem,
            device_id=device, device_id_type=MESH,
        )
        copy.start()
        return copy

    loads = [
        pltpu.make_async_copy(tok_in, tok.at[0, 0, 0, 0], own_sem.at[0]),
        pltpu.make_async_copy(cot_in, tok.at[0, 0, 0, 1], own_sem.at[1]),
        pltpu.make_async_copy(routed_in.at[me], routed.at[me], own_sem.at[2]),
    ]
    weights = []
    for j in range(4):
        cols = pl.ds(j * 256, 256)
        weights.append(pltpu.make_async_copy(wg_in.at[:, cols], wg.at[j], own_sem.at[3 + j]))
        weights.append(pltpu.make_async_copy(wu_in.at[:, cols], wu.at[j], own_sem.at[7 + j]))
        weights.append(pltpu.make_async_copy(wd_in.at[cols], wd.at[j], own_sem.at[11 + j]))
    for copy in loads + weights:
        copy.start()

    barrier = pltpu.get_barrier_semaphore()

    def greet(d, carry):
        pl.semaphore_signal(
            barrier, inc=1, device_id=plane(lax.rem(me + d, 32)), device_id_type=MESH
        )
        return carry

    lax.fori_loop(1, 32, greet, 0)
    for step in (1, 2, 3):
        pl.semaphore_signal(barrier, inc=1, device_id=column(step), device_id_type=MESH)
    pl.semaphore_wait(barrier, 34)

    n_tok = [0]

    def send_tok(src, dst_index, device):
        sem = tok_s.at[n_tok[0]]
        n_tok[0] += 1
        sent.append(send(src, tok.at[dst_index], sem, tok_r.at[dst_index], device))

    def wait_tok(*index):
        landed(tok.at[index], tok_r.at[index])

    def cross(db, da):
        for arr in (0, 1):
            send_tok(tok.at[0, db, da, arr], (1, db, da, arr), partner)

    def second_axis(da):
        for arr in (0, 1):
            send_tok(tok.at[0, 0, da, arr], (0, 3, da, arr), plane(holder(0, da * 0, 1)))
            send_tok(tok.at[0, 0, da, 1 - arr], (0, 1, da, 1 - arr), plane(holder(0, 0, 3)))

    own = (tok_in, cot_in)
    for arr in (0, 1):
        send_tok(own[arr], (0, 0, 3, arr), plane(holder(0, 1, 0)))
        send_tok(own[1 - arr], (0, 0, 1, 1 - arr), plane(holder(0, 3, 0)))
    for arr in (0, 1):
        send_tok(own[arr], (1, 0, 0, arr), partner)

    def send_routed(d, carry):
        target = lax.rem(me + d, 32)
        pltpu.make_async_remote_copy(
            src_ref=routed_in.at[target], dst_ref=routed.at[me],
            send_sem=routed_s.at[d], recv_sem=routed_r.at[me],
            device_id=plane(target), device_id_type=MESH,
        ).start()
        return carry

    lax.fori_loop(1, 32, send_routed, 0)

    prod[:, 2 * HALF :, :] = jnp.zeros((2, 384 - 2 * HALF, 256), BF)
    for copy in loads:
        copy.wait()
    second_axis(0)
    wait_tok(0, 0, 3, 0)
    send_tok(tok.at[0, 0, 3, 0], (0, 0, 2, 0), plane(holder(0, 1, 0)))
    wait_tok(0, 0, 1, 1)
    send_tok(tok.at[0, 0, 1, 1], (0, 0, 2, 1), plane(holder(0, 3, 0)))
    wait_tok(0, 0, 1, 0)
    cross(0, 1)
    second_axis(1)
    wait_tok(0, 0, 3, 1)
    cross(0, 3)
    second_axis(3)

    def wait_routed(d, carry):
        source = lax.rem(me + d, 32)
        landed(routed.at[source], routed_r.at[source])
        return carry

    lax.fori_loop(1, 32, wait_routed, 0)
    for copy in weights:
        copy.wait()
    wait_tok(0, 0, 2, 0)
    wait_tok(0, 0, 2, 1)
    cross(0, 2)
    second_axis(2)

    def relay_tokens(da):
        wait_tok(0, 3, da, 0)
        send_tok(tok.at[0, 3, da, 0], (0, 2, da, 0), plane(holder(0, 0, 1)))
        wait_tok(0, 1, da, 1)
        send_tok(tok.at[0, 1, da, 1], (0, 2, da, 1), plane(holder(0, 0, 3)))
        wait_tok(0, 1, da, 0)
        cross(1, da)
        wait_tok(0, 3, da, 1)
        cross(3, da)

    def finish_tokens(da):
        wait_tok(0, 2, da, 0)
        wait_tok(0, 2, da, 1)
        cross(2, da)

    early = (
        lax.broadcasted_iota(jnp.int32, (128, 128), 0)
        < lax.broadcasted_iota(jnp.int32, (128, 128), 1)
    )
    early = jnp.where(early, 1.0, 0.0).astype(BF)
    row_of = lax.broadcasted_iota(jnp.int32, (HALF, 128), 0).astype(F32)
    outs = []

    def store(src, dst):
        copy = pltpu.make_async_copy(src, dst, out_s.at[len(outs)])
        copy.start()
        outs.append(copy)

    def gather(c):
        db = ORDER[c]
        for da in range(4):
            for arr in (0, 1):
                wait_tok(1, db, da, arr)
        for side in (0, 1):
            weight = jnp.zeros((HALF, 1), F32)
            for i in range(4):
                line = routed[holder(side, i, db)]
                member = line > 0
                rank = mm(jnp.where(member, 1.0, 0.0).astype(BF), early)
                target = jnp.where(member, rank + float(CAP * i), -1.0)
                hit = jnp.broadcast_to(target[0:1], (HALF, 128)) == row_of
                pick[:, i * 128 : (i + 1) * 128] = jnp.where(hit, 1.0, 0.0).astype(BF)
                weight += jnp.sum(
                    jnp.where(hit, jnp.broadcast_to(line[0:1], (HALF, 128)), 0.0),
                    axis=1, keepdims=True,
                )
            g_rows[c, side] = jnp.broadcast_to(weight, (HALF, 128))

            def columns(n, carry):
                cols = pl.ds(pl.multiple_of(n * 256, 256), 256)
                x = tok[side, db, :, 0, :, cols].reshape(512, 256)
                y = tok[side, db, :, 1, :, cols].reshape(512, 256)
                xr[c, side, :, cols] = mm(pick[...], x).astype(BF)
                rows = mm(pick[...], y)
                dyr[side, :, cols] = rows.astype(BF)
                g = g_rows[c, side]
                sdy[c, side, :, cols] = (rows * jnp.concatenate([g, g], axis=1)).astype(BF)
                return carry

            lax.fori_loop(0, 4, columns, 0)
        store(xr.at[c], xr_out.at[c])
        store(sdy.at[c], sdy_out.at[c])

    rs_sent = [[], [], [], []]

    def partial(c):
        p = c % 2
        if c >= 2:
            for copy in rs_sent[c - 2]:
                copy.wait_send()
        x_rows = xr.at[c]
        for rel in (2, 3, 1, 0):
            j = lax.rem(z + rel, 4)
            x = x_rows[...].reshape(2 * HALF, 1024)
            part[p, rel, :, 0] = mm(x, wg[j]).astype(BF).reshape(2, HALF, 256)
            part[p, rel, :, 1] = mm(x, wu[j]).astype(BF).reshape(2, HALF, 256)
            y = dyr[...].reshape(2 * HALF, 1024)
            part[p, rel, :, 2] = mm_nt(y, wd[j]).astype(BF).reshape(2, HALF, 256)
            if rel == 2:
                rs_sent[c] += [
                    send(part.at[p, 2, 0], r1.at[c, 0], r1_s.at[c, 0], r1_r.at[c, 0], column(3)),
                    send(part.at[p, 2, 1], r1.at[c, 1], r1_s.at[c, 1], r1_r.at[c, 1], column(1)),
                ]
            if rel == 3:
                rs_sent[c].append(send(
                    part.at[p, 3, 1], r2.at[c, 0, 1], r2_s.at[c, 0, 1], r2_r.at[c, 0, 1], column(3)
                ))
            if rel == 1:
                rs_sent[c].append(send(
                    part.at[p, 1, 0], r2.at[c, 1, 0], r2_s.at[c, 1, 0], r2_r.at[c, 1, 0], column(1)
                ))

    def add_on(c):
        p = c % 2
        for way, rel, half, step in ((0, 3, 0, 3), (1, 1, 1, 1)):
            landed(r1.at[c, way], r1_r.at[c, way])
            total = part[p, rel, half].astype(F32) + r1[c, way].astype(F32)
            part[p, rel, half] = total.astype(BF)
            rs_sent[c].append(send(
                part.at[p, rel, half], r2.at[c, way, half],
                r2_s.at[c, way, half], r2_r.at[c, way, half], column(step),
            ))

    def finish(c):
        p = c % 2
        for way in (0, 1):
            for half in (0, 1):
                landed(r2.at[c, way, half], r2_r.at[c, way, half])
        for half in (0, 1):

            def block(i, carry):
                rows = pl.ds(pl.multiple_of(i * 16, 16), 16)

                def total(arr):
                    return (
                        part[p, 0, half, arr, rows].astype(F32)
                        + r2[c, 0, half, arr, rows].astype(F32)
                        + r2[c, 1, half, arr, rows].astype(F32)
                    )

                gate_pre, up_pre, back = total(0), total(1), total(2)
                g = g_rows[c, half, rows]
                g = jnp.concatenate([g, g], axis=1)
                sig = jax.nn.sigmoid(gate_pre)
                swish = gate_pre * sig
                hidden = (swish * up_pre).astype(BF)
                product = back * hidden.astype(F32)
                grad_hidden = g * back
                slope = sig * (1.0 + gate_pre * (1.0 - sig))
                act[c, 0, half, 0, rows] = hidden
                act[c, 0, half, 1, rows] = (grad_hidden * up_pre * slope).astype(BF)
                act[c, 0, half, 2, rows] = (grad_hidden * swish).astype(BF)
                high = product.astype(BF)
                at = pl.ds(pl.multiple_of(half * HALF + i * 16, 16), 16)
                prod[0, at] = high
                prod[1, at] = (product - high.astype(F32)).astype(BF)
                return carry

            lax.fori_loop(0, HALF // 16, block, 0)
        for half in (0, 1):
            sent.append(send(
                act.at[c, 0, half], act.at[c, 3, half],
                ag_s.at[c, half], ag_r.at[c, 3, half], column(1),
            ))
            sent.append(send(
                act.at[c, 0, 1 - half], act.at[c, 1, 1 - half],
                ag_s.at[c, 3 - half], ag_r.at[c, 1, 1 - half], column(3),
            ))
        ones = jnp.ones((8, 256), BF)
        gates[c, 0] = mm_nt(ones, prod[0]) + mm_nt(ones, prod[1])
        for step in (1, 2, 3):
            sent.append(send(
                gates.at[c, 0], gates.at[c, 4 - step],
                gates_s.at[c, step], gates_r.at[c, 4 - step], column(step),
            ))
        store(act.at[c, 0], act_out.at[z, c])

    def relay(c):
        landed(act.at[c, 3, 0], ag_r.at[c, 3, 0])
        sent.append(send(
            act.at[c, 3, 0], act.at[c, 2, 0], ag_s.at[c, 4], ag_r.at[c, 2, 0], column(1)
        ))
        landed(act.at[c, 1, 1], ag_r.at[c, 1, 1])
        sent.append(send(
            act.at[c, 1, 1], act.at[c, 2, 1], ag_s.at[c, 5], ag_r.at[c, 2, 1], column(3)
        ))

    lane = lax.broadcasted_iota(jnp.int32, (PAD, HALF), 1)
    sub = lax.broadcasted_iota(jnp.int32, (PAD, HALF), 0)
    spread = jnp.concatenate(
        [
            jnp.where((lane == sub + CAP * i) & (sub < CAP), 1.0, 0.0)
            for i in range(4)
        ],
        axis=0,
    ).astype(BF)
    back_copies = []

    def give_back(c):
        for rel, half in ((3, 1), (1, 0), (2, 0), (2, 1)):
            landed(act.at[c, rel, half], ag_r.at[c, rel, half])
        for rel in (1, 2, 3):
            landed(gates.at[c, rel], gates_r.at[c, rel])
            store(act.at[c, rel], act_out.at[lax.rem(z + rel, 4), c])

        def columns(n, carry):
            at = pl.ds(pl.multiple_of(n * 256, 256), 256)
            total = jnp.zeros((2 * HALF, 256), F32)
            for rel in range(4):
                j = lax.rem(z + rel, 4)
                gate = act[c, rel, :, 1].reshape(2 * HALF, 256)
                up = act[c, rel, :, 2].reshape(2 * HALF, 256)
                total += mm_nt(gate, wg[j, at]) + mm_nt(up, wu[j, at])
            inp[:, :, at] = total.astype(BF).reshape(2, HALF, 256)
            return carry

        lax.fori_loop(0, 4, columns, 0)
        level = lax.broadcasted_iota(jnp.int32, (8, 384), 0)
        lines = jnp.zeros((8, 384), F32)
        for rel in range(4):
            lines = jnp.where(level == 4 + rel, gates[c, rel], lines)
        mask = lax.broadcasted_iota(jnp.int32, (8, 128), 1) < CAP
        for half in (0, 1):
            for n in range(4):
                at = pl.ds(n * 256, 256)
                wide = mm(spread, inp[half, :, at])
                for i in range(4):
                    k = half * 4 + i
                    block = wide[PAD * i : PAD * (i + 1)]
                    if n == 0:
                        turn = (384 - CAP * k) % 384
                        line = pltpu.roll(lines, turn, 1) if turn else lines
                        line = jnp.where(mask, line[:, :128], 0.0)
                        line = jnp.concatenate([line, jnp.zeros((8, 128), F32)], axis=1)
                        block = jnp.concatenate([block[:32], block[32:] + line], axis=0)
                    ret[c, k, :, at] = block.astype(BF)
            for i in range(4):
                k = half * 4 + i
                if c == 0 and k == 0:
                    store(ret.at[c, k], ret_out.at[me])
                else:
                    sent.append(send(
                        ret.at[c, k], ret_out.at[me], ret_s.at[c, k], ret_r.at[me],
                        plane(holder(half, i, ORDER[c])),
                    ))

    gather(0)
    partial(0)
    relay_tokens(0)
    add_on(0)
    relay_tokens(1)
    finish(0)
    relay_tokens(3)
    relay(0)
    relay_tokens(2)
    gather(1)
    partial(1)
    finish_tokens(0)
    finish_tokens(1)
    add_on(1)
    finish_tokens(3)
    finish_tokens(2)
    gather(2)
    partial(2)
    give_back(0)
    finish(1)
    add_on(2)
    relay(1)
    gather(3)
    partial(3)
    finish(2)
    add_on(3)
    relay(2)
    give_back(1)
    finish(3)
    give_back(2)
    relay(3)
    give_back(3)

    def wait_back(d, carry):
        source = lax.rem(me + d, 32)
        landed(ret_out.at[source], ret_r.at[source])
        return carry

    lax.fori_loop(1, 32, wait_back, 0)

    def wait_routed_sent(d, carry):
        target = lax.rem(me + d, 32)
        pltpu.make_async_copy(routed_in.at[target], routed_in.at[target], routed_s.at[d]).wait()
        return carry

    lax.fori_loop(1, 32, wait_routed_sent, 0)
    for copy in rs_sent[2] + rs_sent[3] + sent:
        copy.wait_send()
    for copy in outs:
        copy.wait()


def layer(tokens, cotangent, routed, wg, wu, wd):
    any_space = pl.BlockSpec(memory_space=pl.ANY)
    dma = pltpu.SemaphoreType.DMA
    vmem = pltpu.VMEM
    return pl.pallas_call(
        layer_kernel,
        out_shape=(
            jax.ShapeDtypeStruct((4, 2, HALF, 1024), BF),
            jax.ShapeDtypeStruct((4, 2, HALF, 1024), BF),
            jax.ShapeDtypeStruct((4, 4, 2, 3, HALF, 256), BF),
            jax.ShapeDtypeStruct((EXPERTS, PAD, 1024), BF),
        ),
        in_specs=[any_space] * 6,
        out_specs=(any_space,) * 4,
        scratch_shapes=[
            vmem((2, 4, 4, 2, 128, 1024), BF),
            vmem((4, 1024, 256), BF),
            vmem((4, 1024, 256), BF),
            vmem((4, 256, 1024), BF),
            vmem((EXPERTS, 8, 128), F32),
            vmem((HALF, 512), BF),
            vmem((4, 2, HALF, 128), F32),
            vmem((4, 2, HALF, 1024), BF),
            vmem((4, 2, HALF, 1024), BF),
            vmem((2, HALF, 1024), BF),
            vmem((2, 4, 2, 3, HALF, 256), BF),
            vmem((4, 2, 3, HALF, 256), BF),
            vmem((4, 2, 2, 3, HALF, 256), BF),
            vmem((4, 4, 2, 3, HALF, 256), BF),
            vmem((2, 384, 256), BF),
            vmem((4, 4, 8, 384), F32),
            vmem((2, HALF, 1024), BF),
            vmem((4, 8, PAD, 1024), BF),
            dma((15,)),
            dma((62,)),
            dma((2, 4, 4, 2)),
            dma((EXPERTS,)),
            dma((EXPERTS,)),
            dma((4, 2)),
            dma((4, 2)),
            dma((4, 2, 2)),
            dma((4, 2, 2)),
            dma((4, 6)),
            dma((4, 4, 2)),
            dma((4, 4)),
            dma((4, 4)),
            dma((4, 8)),
            dma((EXPERTS,)),
            dma((25,)),
        ],
        compiler_params=pltpu.CompilerParams(
            collective_id=0, has_side_effects=True, vmem_limit_bytes=67043328
        ),
        name="layer",
    )(tokens, cotangent, routed, wg, wu, wd)


def weights_kernel(xr_ref, sdy_ref, act_ref, gate_ref, up_ref, down_ref):
    rows = 8 * HALF
    hidden = act_ref[0, :, :, 0].reshape(rows, 256)
    gate = act_ref[0, :, :, 1].reshape(rows, 256)
    up = act_ref[0, :, :, 2].reshape(rows, 256)
    for n in range(4):
        at = pl.ds(n * 256, 256)
        x = xr_ref[:, :, :, at].reshape(rows, 256)
        y = sdy_ref[:, :, :, at].reshape(rows, 256)
        gate_ref[at, :] = mm_tn(x, gate)
        up_ref[at, :] = mm_tn(x, up)
        down_ref[:, at] = mm_tn(hidden, y)


def weight_grads(xr, sdy, act):
    whole = pl.BlockSpec((4, 2, HALF, 1024), lambda j: (0, 0, 0, 0))
    out = jax.ShapeDtypeStruct((1024, 1024), F32)
    return pl.pallas_call(
        weights_kernel,
        grid=(4,),
        out_shape=(out, out, out),
        in_specs=[
            whole,
            whole,
            pl.BlockSpec((1, 4, 2, 3, HALF, 256), lambda j: (j, 0, 0, 0, 0, 0)),
        ],
        out_specs=(
            pl.BlockSpec((1024, 256), lambda j: (0, j)),
            pl.BlockSpec((1024, 256), lambda j: (0, j)),
            pl.BlockSpec((256, 1024), lambda j: (j, 0)),
        ),
        compiler_params=pltpu.CompilerParams(vmem_limit_bytes=60000000),
        name="weight_grads",
    )(xr, sdy, act)


def shards(tokens, cotangent, gate_probs, expert_ids, gate_weight, up_weight, down_weight):
    count, width = tokens.shape
    wg, wu, wd = gate_weight[0], up_weight[0], down_weight[0]
    columns = jnp.arange(EXPERTS, dtype=jnp.int32)
    chosen = expert_ids[:, :, None] == columns[None, None, :]
    local = jnp.sum(jnp.where(chosen, gate_probs[:, :, None].astype(F32), 0.0), axis=1)
    routed = jnp.broadcast_to(local.T[:, None, :], (EXPERTS, 8, count))
    xr, sdy, act, ret = layer(tokens, cotangent, routed, wg, wu, wd)
    grad_gate, grad_up, grad_down = weight_grads(xr, sdy, act)
    before = (jnp.arange(count)[:, None] < jnp.arange(count)[None, :]).astype(BF)
    slots = jnp.arange(PAD, dtype=F32)
    local_rank = dot32("tu,te->ue", before, (local > 0).astype(BF))
    place = (local_rank[:, :, None] == slots[None, None, :]) & (local[:, :, None] > 0)
    gate_table = jnp.sum(ret[:, CAP:, :PAD].astype(F32), axis=1)
    by_expert = jnp.sum(jnp.where(place, gate_table[None], 0.0), axis=2)
    grad_gates = jnp.sum(jnp.where(chosen, by_expert[:, None, :], 0.0), axis=2)
    place = place.astype(BF).reshape(count, EXPERTS * PAD)
    grad_tokens = dot32("tr,rd->td", place, ret.reshape(EXPERTS * PAD, width)).astype(BF)
    return (grad_tokens, grad_gates, grad_gate[None], grad_up[None], grad_down[None])


def solution(mesh):
    placed = (
        P("expert", "dp"),
        P("expert", "dp"),
        P("expert", None),
        P("expert", None),
        P("expert", "dp", None),
        P("expert", "dp", None),
        P("expert", None, "dp"),
    )
    return jax.shard_map(
        shards,
        mesh=mesh,
        in_specs=placed,
        out_specs=(
            P("expert", "dp"),
            P("expert", None),
            P("expert", "dp", None),
            P("expert", "dp", None),
            P("expert", None, "dp"),
        ),
        check_vma=False,
    )
```
